128 devices in a mesh: det: 8 (over y, core), patch: 16 (over z, x).
Axes of the slice: x: 4, y: 4, z: 4, core: 2. Of those that a mesh axis runs over, the one named last changes fastest.
Arguments:
- exposure: bfloat16 [32768, 4096], P(('det', 'patch')), may hold values from -8 to 8
- block_dest: int32 [4096], P(('det', 'patch')), may hold values from 0 to 4095, as said below
- band_offset: int32 [4096], P(('det', 'patch')), may hold values from -8 to 8
- col_shift: float32 [4096], P(('det', 'patch')), may hold values from 0.05 to 0.95
- block_weight: float32 [4096], P(('det', 'patch')), may hold values from 0.5 to 4
- basis_width: float32 [3], replicated, may hold values from 1 to 5
- kernel_fit: float32 [128, 3, 6], P(('det', 'patch')), may hold values from -3 to 3
- fit_owner: int32 [1], replicated, may hold values from 0 to 127
Outputs:
- matched: bfloat16 [32768, 4096], P(('det', 'patch'))
- coverage: float32 [4096], P(('det', 'patch'))
The draws below stay inside these ranges and needn't reach their ends.
Inputs may be any that keep to these rules, and one draw needn't show every extreme that they name: `block_dest`: block b of device d (b in d * 32 .. d * 32 + 31) lands in a slot of a device of d's det group (slots d' 32 .. d' 32 + 31 belong to device d'); no device sends more than 3 of its blocks to one device, and every device sends exactly 3 to some device.
All inputs are finite; a program needn't handle non-finite values.
Results may differ from the reference program's by a relative error of at most 0.013.
Values may be sent and summed in bfloat16 or wider, within the bound.
A program may use at most 448 MiB of HBM per device.

```python
import math
import jax
import jax.numpy as jnp
from jax import lax

W = 4096
TAPS = 31
BASES = 3
NPOLY = 6
BLK = 8
BPD = 32
ROWS_DEV = 256
BLOCKS = 4096
ROWS = 32768
N_PATCH = 16
DEVICES = 128


def draw_block_dest(key, part):
    mean_count = BPD // N_PATCH
    counts = jnp.full((N_PATCH,), mean_count, jnp.int32).at[0].add(1).at[1].add(-1)

    def one_device(device_key, device_index):
        key_order, key_shuffle, key_slot = jax.random.split(device_key, 3)
        peer_order = jax.random.permutation(key_order, N_PATCH)
        peer_list = jnp.repeat(peer_order, counts, total_repeat_length=BPD)
        peer_list = jax.random.permutation(key_shuffle, peer_list)
        slot_list = jax.random.randint(key_slot, (BPD,), 0, BPD)
        group_index = device_index // N_PATCH
        return (group_index * N_PATCH + peer_list) * BPD + slot_list
    device_keys = jax.random.split(jax.random.fold_in(key, 17), DEVICES)
    routes = jax.vmap(one_device)(device_keys, jnp.arange(DEVICES))
    return routes.reshape(-1).astype(jnp.int32)


def plant(drawn, stream_key, least, largest):
    extent = drawn.shape
    index_at = [jax.random.randint(jax.random.fold_in(stream_key, axis), (), 0, extent[axis]) for axis in range(len(extent))]
    drawn = drawn.at[tuple(index_at)].set(least)
    longest = extent.index(max(extent))
    index_at[longest] = (index_at[longest] + 1) % extent[longest]
    return drawn.at[tuple(index_at)].set(largest)


def level_of(key, dims, cuts, least, largest):
    def one(dim, shards_of):
        draws = jax.random.uniform(jax.random.fold_in(jax.random.fold_in(key, 6), dim), (shards_of,), jnp.float32, least / len(cuts), largest / len(cuts))
        return jnp.repeat(jnp.exp(draws), dims[dim] // shards_of).reshape((-1,) + (1,) * (len(dims) - dim - 1))

    loudness = one(*cuts[0])
    for cut in cuts[1:]:
        loudness = loudness * one(*cut)
    return loudness


def normal_values(stream_key, dims, deviation, bound, cuts=(), dtype=jnp.bfloat16):
    loudness = level_of(stream_key, dims, cuts, -0.22, 0.18) if cuts else 1.0
    values = jax.random.normal(stream_key, dims, jnp.float32) * deviation * loudness
    return jnp.minimum(jnp.maximum(values, -bound), bound).astype(dtype)


def setup_inputs(seed: int = 0) -> dict:
    key_list = jax.random.split(jax.random.key(seed), 9)
    return {
        "exposure": normal_values(key_list[0], (ROWS, W), 1.0, 8.0, ((0, 128),)),
        "block_dest": draw_block_dest(jax.random.fold_in(key_list[8], 71), 0),
        "band_offset": plant(jax.random.randint(key_list[2], (BLOCKS,), -8, 9), jax.random.fold_in(key_list[2], 1), -8, 8).astype(jnp.int32),
        "col_shift": jnp.clip(0.05 + 0.9 * jax.random.uniform(key_list[3], (BLOCKS,), jnp.float32) ** level_of(key_list[3], (BLOCKS,), ((0, 128),), -0.2, 0.2), 0.05, 0.95),
        "block_weight": jnp.clip(jnp.exp(math.log(4.0) - 2.0794415 * jax.random.uniform(key_list[4], (BLOCKS,), jnp.float32) ** level_of(key_list[4], (BLOCKS,), ((0, 128),), -0.2, 0.2)), 0.5, 4.0),
        "basis_width": jnp.clip(jnp.exp(jax.random.uniform(key_list[5], (BASES,), jnp.float32, math.log(1.0), math.log(5.0))), 1.0, 5.0),
        "kernel_fit": normal_values(key_list[6], (DEVICES, BASES, NPOLY), 0.5, 3.0, ((0, 128),), jnp.float32),
        "fit_owner": jax.random.randint(key_list[7], (1,), 0, DEVICES).astype(jnp.int32),
    }


def lanczos(position):
    return jnp.sinc(position) * jnp.sinc(position / 3.0)


def resample_blocks(source_rows, offsets, shifts, weights):
    col_count = source_rows.shape[2]
    column_margin = 16
    padded = jnp.pad(source_rows, ((0, 0), (0, 0), (column_margin, column_margin)))
    summed = jnp.zeros(source_rows.shape, jnp.float32)
    for offset_tap in range(-2, 4):
        coeffs = lanczos(offset_tap - shifts)
        starts = (offsets + offset_tap + column_margin).astype(jnp.int32)
        picked = jax.vmap(lambda source_block, start_col: lax.dynamic_slice_in_dim(source_block, start_col, col_count, 1))(padded, starts)
        summed = summed + coeffs[:, None, None] * picked.astype(jnp.float32)
    return summed * weights[:, None, None]


def gaussian_taps(basis_width):
    half_span = (TAPS - 1) // 2
    positions = jnp.arange(TAPS).astype(jnp.float32) - half_span
    profile = jnp.exp(-(positions[None, :] ** 2) / (2.0 * basis_width[:, None] ** 2))
    return profile / jnp.sum(profile, axis=1, keepdims=True)


def poly_field(coeff_row, row_pos, col_pos):
    yy_pos = row_pos[:, None]
    xx_pos = col_pos[None, :]
    return (coeff_row[0] + coeff_row[1] * xx_pos + coeff_row[2] * yy_pos + coeff_row[3] * xx_pos * xx_pos
            + coeff_row[4] * xx_pos * yy_pos + coeff_row[5] * yy_pos * yy_pos)


def reference(exposure, block_dest, band_offset, col_shift, block_weight, basis_width, kernel_fit, fit_owner):
    source_blocks = exposure.reshape(BLOCKS, BLK, W)
    weighted = resample_blocks(source_blocks, band_offset, col_shift, block_weight).astype(jnp.bfloat16)
    coadd_sum = jax.ops.segment_sum(weighted.astype(jnp.float32), block_dest, num_segments=BLOCKS)
    coverage = jax.ops.segment_sum(block_weight, block_dest, num_segments=BLOCKS)
    image = (coadd_sum / jnp.maximum(coverage, 1.0)[:, None, None]).astype(jnp.bfloat16).reshape(ROWS, W)
    profile = gaussian_taps(basis_width)
    col_taps = profile.astype(jnp.bfloat16).astype(jnp.float32)
    coeff = lax.dynamic_index_in_dim(kernel_fit, fit_owner[0], 0, keepdims=False)
    half_span = (TAPS - 1) // 2
    padded_image = jnp.pad(image, ((half_span, half_span), (half_span, half_span)))
    col_pos = 2.0 * jnp.arange(W).astype(jnp.float32) / (W - 1) - 1.0

    def one_stripe(stripe_index):
        start_row = stripe_index * ROWS_DEV
        window = lax.dynamic_slice_in_dim(padded_image, start_row, ROWS_DEV + 2 * half_span, 0).astype(jnp.float32)
        row_pos = 2.0 * (start_row + jnp.arange(ROWS_DEV)).astype(jnp.float32) / (ROWS - 1) - 1.0
        result = jnp.zeros((ROWS_DEV, W), jnp.float32)
        for basis_index in range(BASES):
            colconv = jnp.zeros((ROWS_DEV + 2 * half_span, W), jnp.float32)
            for tap_index in range(TAPS):
                colconv = colconv + col_taps[basis_index, tap_index] * window[:, tap_index:tap_index + W]
            rowconv = jnp.zeros((ROWS_DEV, W), jnp.float32)
            for tap_index in range(TAPS):
                rowconv = rowconv + profile[basis_index, tap_index] * colconv[tap_index:tap_index + ROWS_DEV]
            result = result + poly_field(coeff[basis_index], row_pos, col_pos) * rowconv
        return result.astype(jnp.bfloat16)

    stripes = lax.map(one_stripe, jnp.arange(DEVICES).astype(jnp.int32))
    return stripes.reshape(ROWS, W), coverage
```

```python
import functools

import jax
import jax.numpy as jnp
from jax import lax
from jax.experimental import pallas as pl
from jax.experimental.pallas import tpu as pltpu
from jax.sharding import PartitionSpec as P

MESH = pl.DeviceIdType.MESH
TAPS = 31
HALF = 15
BASES = 3
NPOLY = 6
COLS = 4096
CHUNKS = 8
WIDTH = COLS // CHUNKS
TILES = WIDTH // 128
BLOCKS = 32
ROWS = 256
PEERS = 16
GROUPS = 8
RANKS = 3
SLOTS = RANKS * PEERS
PACKED = SLOTS * 8
EDGE = 16
ALL_ROWS = ROWS * PEERS * GROUPS
FIT_LANE = 2
F32 = jnp.float32
BF16 = jnp.bfloat16


def iota(shape, dim):
    return lax.broadcasted_iota(jnp.int32, shape, dim)


def gaussian(distance, width, norm):
    value = jnp.exp(-(distance * distance) / (2.0 * width * width)) / norm
    return jnp.where(jnp.abs(distance) <= HALF, value, 0.0)


def kernel(
    coef_ref, offset_ref, width_ref, owner_ref, rows_ref, exposure_ref, out_ref, cover_ref,
    padded, weighted, packed, arrived, meta_out, meta_in, fit_out, fit_in, edges,
    pack_mat, row_mat, edge_mat, band_mat, rowconv, y_cols, edge_scale, fit_sum,
    load_sem, fit_send, fit_recv, meta_send, meta_recv, bulk_send, bulk_recv, edge_send, edge_recv,
):
    det = lax.axis_index("det")
    pat = lax.axis_index("patch")
    dev = det * PEERS + pat
    after = lax.rem(dev + 1, PEERS * GROUPS)
    before = lax.rem(dev + PEERS * GROUPS - 1, PEERS * GROUPS)
    after_id = (after // PEERS, lax.rem(after, PEERS))
    before_id = (before // PEERS, lax.rem(before, PEERS))

    barrier = pltpu.get_barrier_semaphore()

    @pl.loop(1, PEERS)
    def _(step):
        pl.semaphore_signal(
            barrier, inc=1, device_id=(det, lax.rem(pat + step, PEERS)), device_id_type=MESH
        )

    @pl.loop(1, GROUPS)
    def _(step):
        pl.semaphore_signal(
            barrier, inc=1, device_id=(lax.rem(det + step, GROUPS), pat), device_id_type=MESH
        )

    pl.semaphore_signal(barrier, inc=1, device_id=after_id, device_id_type=MESH)
    pl.semaphore_signal(barrier, inc=1, device_id=before_id, device_id_type=MESH)

    load = pltpu.make_async_copy(exposure_ref, padded.at[:, :, 128 : 128 + COLS], load_sem)
    load.start()
    padded[:, :, 0:128] = jnp.zeros((BLOCKS, 8, 128), BF16)
    padded[:, :, 128 + COLS :] = jnp.zeros((BLOCKS, 8, 128), BF16)

    peer = rows_ref[0:1, :]
    slot = rows_ref[1:2, :]
    weight = rows_ref[2:3, :]
    fit_row = rows_ref[3:4, 0:128]
    lane = iota((1, ROWS), 1)
    phase = lax.rem(lane, 8).astype(F32)
    row_i = iota((ROWS, ROWS), 0)
    col_i = iota((ROWS, ROWS), 1)
    peer_col = jnp.sum(jnp.where(row_i == col_i, peer, 0.0), axis=1, keepdims=True)
    earlier = (row_i // 8) < (col_i // 8)
    same = jnp.where(jnp.logical_and(peer_col == peer, earlier), 1.0, 0.0)
    rank = jnp.sum(same, axis=0, keepdims=True) * 0.125
    target = rank * 128.0 + peer * 8.0 + phase
    select = jnp.where(iota((PACKED, ROWS), 0).astype(F32) == target, 1.0, 0.0)
    pack_mat[...] = select.astype(BF16)
    row_col = jnp.sum(select * (slot * 8.0 + phase + 1.0), axis=1, keepdims=True)
    weight_col = jnp.sum(select * weight, axis=1, keepdims=True)

    mine = jnp.where(owner_ref[0] == dev, 1.0, 0.0)
    fit_out[...] = jnp.broadcast_to(jnp.where(mine > 0.5, fit_row, 0.0), (8, 128))
    fit_in[det] = fit_out[...]

    pl.semaphore_wait(barrier, PEERS - 1 + GROUPS - 1 + 2)

    @pl.loop(1, GROUPS)
    def _(step):
        pltpu.make_async_remote_copy(
            fit_out, fit_in.at[det], fit_send, fit_recv,
            device_id=(lax.rem(det + step, GROUPS), pat), device_id_type=MESH,
        ).start()

    load.wait()

    def resample(chunk):
        start = pl.multiple_of(chunk * WIDTH, 128)

        @pl.loop(0, BLOCKS)
        def _(block):
            source = padded[block, :, pl.ds(start, WIDTH + 256)].astype(F32)
            offset = offset_ref[block]
            turn = lax.rem(128 - offset, 128)
            ahead = offset >= 0
            lanes = iota((8, 128), 1)
            moved = lanes + offset
            wraps = jnp.logical_or(moved < 0, moved >= 128)
            turned = [
                pltpu.roll(source[:, t * 128 : (t + 1) * 128], turn, axis=1)
                for t in range(TILES + 2)
            ]
            shifted = []
            for t in range(TILES + 2):
                right = turned[min(t + 1, TILES + 1)]
                left = turned[max(t - 1, 0)]
                shifted.append(jnp.where(wraps, jnp.where(ahead, right, left), turned[t]))
            coefs = [coef_ref[block * 6 + i] for i in range(6)]
            total = [coefs[2] * shifted[t] for t in range(1, TILES + 1)]
            for tap in (-2, -1, 1, 2, 3):
                rolled = [pltpu.roll(value, (128 - tap) % 128, axis=1) for value in shifted]
                for t in range(1, TILES + 1):
                    if tap > 0:
                        value = jnp.where(lanes < 128 - tap, rolled[t], rolled[t + 1])
                    else:
                        value = jnp.where(lanes >= -tap, rolled[t], rolled[t - 1])
                    total[t - 1] = total[t - 1] + coefs[tap + 2] * value
            weighted[block] = jnp.concatenate(total, axis=1).astype(BF16)

        gathered = jnp.dot(
            pack_mat[...], weighted[...].reshape(ROWS, WIDTH), preferred_element_type=F32
        )
        packed[chunk] = gathered.astype(BF16).reshape(RANKS, PEERS, 8, WIDTH)

    def send(chunk):
        pltpu.make_async_copy(
            packed.at[chunk, :, pat], arrived.at[chunk, 0:RANKS, pat], bulk_recv.at[chunk]
        ).start()

        @pl.loop(1, PEERS)
        def _(step):
            other = lax.rem(pat + step, PEERS)
            pltpu.make_async_remote_copy(
                packed.at[chunk, :, other], arrived.at[chunk, 0:RANKS, pat],
                bulk_send.at[chunk], bulk_recv.at[chunk],
                device_id=(det, other), device_id_type=MESH,
            ).start()

    resample(0)
    whole = fit_in.at[0 : GROUPS - 1]
    pltpu.make_async_copy(whole, whole, fit_recv).wait()
    chosen = jnp.sum(fit_in[...], axis=0)
    lanes_m = iota((PACKED, 128), 1)
    meta = jnp.where(lanes_m == 0, row_col, jnp.where(lanes_m == 1, weight_col, chosen[0:1, :]))
    meta_out[...] = meta.reshape(RANKS, PEERS, 8, 128)
    pltpu.make_async_copy(meta_out.at[:, pat], meta_in.at[:, pat], meta_recv).start()

    @pl.loop(1, PEERS)
    def _(step):
        other = lax.rem(pat + step, PEERS)
        pltpu.make_async_remote_copy(
            meta_out.at[:, other], meta_in.at[:, pat], meta_send, meta_recv,
            device_id=(det, other), device_id_type=MESH,
        ).start()

    send(0)

    @pl.loop(1, CHUNKS)
    def _(chunk):
        resample(chunk)
        send(chunk)

    span = iota((8, 128), 1).astype(F32) - HALF
    norms = []
    for k in range(BASES):
        value = jnp.exp(-(span * span) / (2.0 * width_ref[k] * width_ref[k]))
        value = jnp.where(span <= HALF, value, 0.0)
        norms.append(jnp.sum(value, axis=1, keepdims=True)[0:1, :])
    across = (iota((512, 256), 0) - 128 - iota((512, 256), 1)).astype(F32)
    for k in range(BASES):
        band_mat[k] = gaussian(across, width_ref[k], norms[k]).astype(BF16)
    y_cols[...] = 2.0 * (dev * ROWS + iota((ROWS, 128), 0)).astype(F32) / (ALL_ROWS - 1) - 1.0
    for k in range(BASES):
        rowconv[k, :, 0:128] = jnp.zeros((ROWS, 128), BF16)
        rowconv[k, :, 128 + COLS :] = jnp.zeros((ROWS, 128), BF16)

    pltpu.make_async_copy(meta_in, meta_in, meta_recv).wait()
    meta_got = meta_in[...].reshape(PACKED, 128)
    got_row = meta_got[:, 0:1] - 1.0
    got_weight = meta_got[:, 1:2]
    lands = jnp.where(got_row == iota((PACKED, ROWS), 1).astype(F32), 1.0, 0.0)
    cover = jnp.sum(lands * got_weight, axis=0, keepdims=True)
    cover_ref[...] = jnp.broadcast_to(cover, (8, ROWS))
    scale = 1.0 / jnp.maximum(cover, 1.0)
    fit_sum[...] = jnp.sum(meta_in[0], axis=0)
    lands = lands.astype(BF16)
    contract = (((1,), (1,)), ((), ()))
    reach = (iota((ROWS, ROWS), 1) - iota((ROWS, ROWS), 0)).astype(F32)
    rim = iota((ROWS, 2 * EDGE), 1)
    rim_at = jnp.where(rim < EDGE, rim - EDGE, rim + ROWS - EDGE)
    rim_reach = (rim_at - iota((ROWS, 2 * EDGE), 0)).astype(F32)
    low_live = jnp.where(dev > 0, 1.0, 0.0)
    high_live = jnp.where(dev < PEERS * GROUPS - 1, 1.0, 0.0)
    rim_live = jnp.where(rim < EDGE, low_live, high_live)
    for k in range(BASES):
        inner = (gaussian(reach, width_ref[k], norms[k]) * scale).astype(BF16)
        spread = lax.dot_general(inner, lands, contract, preferred_element_type=F32)
        row_mat[k * ROWS : (k + 1) * ROWS, 0:PACKED] = spread.astype(BF16)
        outer = gaussian(rim_reach, width_ref[k], norms[k]) * rim_live
        row_mat[k * ROWS : (k + 1) * ROWS, PACKED:] = outer.astype(BF16)
    edge_i = iota((2 * EDGE, ROWS), 0)
    edge_row = jnp.where(edge_i < EDGE, edge_i, edge_i + ROWS - 2 * EDGE)
    picks = jnp.where(edge_row == iota((2 * EDGE, ROWS), 1), 1.0, 0.0)
    edge_mat[...] = lax.dot_general(
        picks.astype(BF16), lands, contract, preferred_element_type=F32
    ).astype(BF16)
    edge_scale[...] = jnp.broadcast_to(
        jnp.sum(picks * scale, axis=1, keepdims=True), (2 * EDGE, 128)
    )

    def edge_copies(chunk):
        return (
            pltpu.make_async_remote_copy(
                edges.at[chunk, 0:2], arrived.at[chunk, RANKS, 2:4],
                edge_send.at[chunk], edge_recv.at[chunk],
                device_id=before_id, device_id_type=MESH,
            ),
            pltpu.make_async_remote_copy(
                edges.at[chunk, 2:4], arrived.at[chunk, RANKS, 0:2],
                edge_send.at[chunk], edge_recv.at[chunk],
                device_id=after_id, device_id_type=MESH,
            ),
        )

    def make_edges(chunk):
        landed = arrived.at[chunk, 0:RANKS]
        pltpu.make_async_copy(landed, landed, bulk_recv.at[chunk]).wait()
        rows = jnp.dot(
            edge_mat[...], arrived[chunk, 0:RANKS].reshape(PACKED, WIDTH),
            preferred_element_type=F32,
        )
        rows = rows * edge_scale[:, 0:1]
        edges[chunk] = rows.astype(BF16).reshape(4, 8, WIDTH)
        for copy in edge_copies(chunk):
            copy.start()

    def row_stage(chunk):
        rims = arrived.at[chunk, RANKS, 0:4]
        pltpu.make_async_copy(rims, rims, edge_recv.at[chunk]).wait()
        got = arrived[chunk, 0:RANKS].reshape(PACKED, WIDTH)
        rim_rows = arrived[chunk, RANKS, 0:4].reshape(2 * EDGE, WIDTH)
        full = jnp.concatenate([got, rim_rows], axis=0)
        at = pl.ds(pl.multiple_of(128 + chunk * WIDTH, 128), WIDTH)
        for k in range(BASES):
            value = jnp.dot(
                row_mat[k * ROWS : (k + 1) * ROWS, :], full, preferred_element_type=F32
            )
            rowconv[k, :, at] = value.astype(BF16)

    fit_now = fit_sum[0:1, :]
    terms = [
        [
            jnp.sum(
                jnp.where(iota((1, 128), 1) == FIT_LANE + k * NPOLY + i, fit_now, 0.0),
                axis=1, keepdims=True,
            )
            for i in range(NPOLY)
        ]
        for k in range(BASES)
    ]

    def col_tile(tile):
        at = pl.multiple_of(tile * 256, 128)
        x = 2.0 * (tile * 256 + iota((1, 256), 1)).astype(F32) / (COLS - 1) - 1.0
        y = y_cols[:, 0:1]
        result = None
        for k in range(BASES):
            value = jnp.dot(
                rowconv[k, :, pl.ds(at, 512)], band_mat[k], preferred_element_type=F32
            )
            a = terms[k]
            level = a[0] + a[1] * x + a[3] * x * x
            slope = a[2] + a[4] * x
            field = level + y * slope + (a[5] * y) * y
            part = field * value
            result = part if result is None else result + part
        out_ref[:, pl.ds(at, 256)] = result.astype(BF16)

    make_edges(0)

    @pl.loop(1, CHUNKS)
    def _(chunk):
        make_edges(chunk)
        row_stage(chunk - 1)

        @pl.when(chunk > 1)
        def _():
            col_tile(2 * chunk - 3)

        col_tile(2 * chunk - 2)

    row_stage(CHUNKS - 1)
    for tile in (2 * CHUNKS - 3, 2 * CHUNKS - 2, 2 * CHUNKS - 1):
        col_tile(tile)

    pltpu.make_async_copy(whole, whole, fit_send).wait()
    sent = meta_out.at[:, 0 : PEERS - 1]
    pltpu.make_async_copy(sent, sent, meta_send).wait()

    @pl.loop(0, CHUNKS)
    def _(chunk):
        gone = packed.at[chunk, :, 0 : PEERS - 1]
        pltpu.make_async_copy(gone, gone, bulk_send.at[chunk]).wait()
        pltpu.make_async_copy(edges.at[chunk], edges.at[chunk], edge_send.at[chunk]).wait()


def shards(
    exposure, block_dest, band_offset, col_shift, block_weight, basis_width, kernel_fit, fit_owner
):
    positions = jnp.arange(-2, 4).astype(F32)[None, :] - col_shift[:, None]
    coefs = jnp.sinc(positions) * jnp.sinc(positions / 3.0) * block_weight[:, None]
    fit_row = jnp.pad(kernel_fit.reshape(1, BASES * NPOLY), ((0, 0), (FIT_LANE, ROWS - FIT_LANE - BASES * NPOLY)))
    peer = block_dest // BLOCKS % PEERS
    slot = block_dest % BLOCKS
    table = jnp.stack([peer.astype(F32), slot.astype(F32), block_weight])
    rows = jnp.concatenate(
        [jnp.repeat(table, 8, axis=1), fit_row, jnp.zeros((4, ROWS), F32)], axis=0
    )
    smem = pl.BlockSpec(memory_space=pltpu.SMEM)
    vmem = pl.BlockSpec(memory_space=pltpu.VMEM)
    matched, cover = pl.pallas_call(
        kernel,
        out_shape=(
            jax.ShapeDtypeStruct((ROWS, COLS), BF16),
            jax.ShapeDtypeStruct((8, ROWS), F32),
        ),
        in_specs=[smem, smem, smem, smem, vmem, pl.BlockSpec(memory_space=pl.ANY)],
        out_specs=(vmem, vmem),
        scratch_shapes=[
            pltpu.VMEM((BLOCKS, 8, COLS + 256), BF16),
            pltpu.VMEM((BLOCKS, 8, WIDTH), BF16),
            pltpu.VMEM((CHUNKS, RANKS, PEERS, 8, WIDTH), BF16),
            pltpu.VMEM((CHUNKS, RANKS + 1, PEERS, 8, WIDTH), BF16),
            pltpu.VMEM((RANKS, PEERS, 8, 128), F32),
            pltpu.VMEM((RANKS, PEERS, 8, 128), F32),
            pltpu.VMEM((8, 128), F32),
            pltpu.VMEM((GROUPS, 8, 128), F32),
            pltpu.VMEM((CHUNKS, 4, 8, WIDTH), BF16),
            pltpu.VMEM((PACKED, ROWS), BF16),
            pltpu.VMEM((BASES * ROWS, PACKED + 2 * EDGE), BF16),
            pltpu.VMEM((2 * EDGE, PACKED), BF16),
            pltpu.VMEM((BASES, 512, 256), BF16),
            pltpu.VMEM((BASES, ROWS, COLS + 256), BF16),
            pltpu.VMEM((ROWS, 128), F32),
            pltpu.VMEM((2 * EDGE, 128), F32),
            pltpu.VMEM((8, 128), F32),
            pltpu.SemaphoreType.DMA,
            pltpu.SemaphoreType.DMA,
            pltpu.SemaphoreType.DMA,
            pltpu.SemaphoreType.DMA,
            pltpu.SemaphoreType.DMA,
            pltpu.SemaphoreType.DMA((CHUNKS,)),
            pltpu.SemaphoreType.DMA((CHUNKS,)),
            pltpu.SemaphoreType.DMA((CHUNKS,)),
            pltpu.SemaphoreType.DMA((CHUNKS,)),
        ],
        compiler_params=pltpu.CompilerParams(
            collective_id=0, has_side_effects=True, vmem_limit_bytes=52 << 20
        ),
        name="coadd_match",
    )(
        coefs.reshape(-1), band_offset, basis_width, fit_owner, rows,
        exposure.reshape(BLOCKS, 8, COLS),
    )
    return matched, cover[0].reshape(BLOCKS, 8)[:, 0]


def solution(mesh):
    row_spec = P(("det", "patch"))
    in_specs = (
        P(("det", "patch"), None), row_spec, row_spec, row_spec, row_spec,
        P(), P(("det", "patch"), None, None), P(),
    )
    out_specs = (P(("det", "patch"), None), row_spec)
    return jax.shard_map(shards, mesh=mesh, in_specs=in_specs, out_specs=out_specs, check_vma=False)
```

```python
import functools

import jax
import jax.numpy as jnp
from jax import lax
from jax.experimental import pallas as pl
from jax.experimental.pallas import tpu as pltpu
from jax.sharding import PartitionSpec as P

MESH = pl.DeviceIdType.MESH
TAPS = 31
HALF = 15
BASES = 3
NPOLY = 6
COLS = 4096
CHUNKS = 8
WINDOW = 3
UNROLL = 16
LEAD = 9
LAG = 2
WIDTH = COLS // CHUNKS
TILES = WIDTH // 128
BLOCKS = 32
ROWS = 256
PEERS = 16
GROUPS = 8
RANKS = 3
SLOTS = RANKS * PEERS
PACKED = SLOTS * 8
EDGE = 16
ALL_ROWS = ROWS * PEERS * GROUPS
FIT_LANE = 6
F32 = jnp.float32
BF16 = jnp.bfloat16


def iota(shape, dim):
    return lax.broadcasted_iota(jnp.int32, shape, dim)


def sinc(value):
    angle = jnp.pi * value
    return jnp.where(value == 0.0, 1.0, jnp.sin(angle) / jnp.where(value == 0.0, 1.0, angle))


def gaussian(distance, width, norm):
    value = jnp.exp(-(distance * distance) / (2.0 * width * width)) / norm
    return jnp.where(jnp.abs(distance) <= HALF, value, 0.0)


def kernel(
    dest_hbm, offset_hbm, shift_hbm, weight_hbm, width_hbm, fit_hbm, owner_ref, exposure_ref,
    out_ref, cover_ref,
    dest_ref, offset_ref, shift_ref, weight_ref, width_ref, fit_ref, small_sem,
    padded, weighted, packed, arrived, meta_out, meta_in, fit_out, fit_in, edges,
    pack_mat, row_mat, edge_mat, band_mat, rowconv, y_cols, edge_scale, coef_table, coef_ref,
    moved, shift_mat, coef_wide,
    load_sem, coef_sem, fit_send, fit_recv, meta_send, meta_recv, bulk_send, bulk_recv, edge_send, edge_recv,
):
    det = lax.axis_index("det")
    pat = lax.axis_index("patch")
    dev = det * PEERS + pat
    after = lax.rem(dev + 1, PEERS * GROUPS)
    before = lax.rem(dev + PEERS * GROUPS - 1, PEERS * GROUPS)
    after_id = (after // PEERS, lax.rem(after, PEERS))
    before_id = (before // PEERS, lax.rem(before, PEERS))

    load = pltpu.make_async_copy(exposure_ref, padded.at[:, :, 128 : 128 + COLS], load_sem)
    load.start()
    smalls = [
        pltpu.make_async_copy(source, target, small_sem.at[i])
        for i, (source, target) in enumerate(
            (
                (dest_hbm, dest_ref), (shift_hbm, shift_ref), (weight_hbm, weight_ref),
                (fit_hbm, fit_ref), (offset_hbm, offset_ref),
                (width_hbm, width_ref),
            )
        )
    ]
    for copy in smalls:
        copy.start()

    barrier = pltpu.get_barrier_semaphore()

    @pl.loop(1, PEERS)
    def _(step):
        pl.semaphore_signal(
            barrier, inc=1, device_id=(det, lax.rem(pat + step, PEERS)), device_id_type=MESH
        )

    @pl.loop(1, GROUPS)
    def _(step):
        pl.semaphore_signal(
            barrier, inc=1, device_id=(lax.rem(det + step, GROUPS), pat), device_id_type=MESH
        )

    pl.semaphore_signal(barrier, inc=1, device_id=after_id, device_id_type=MESH)
    pl.semaphore_signal(barrier, inc=1, device_id=before_id, device_id_type=MESH)

    padded[:, :, 0:128] = jnp.zeros((BLOCKS, 8, 128), BF16)
    padded[:, :, 128 + COLS :] = jnp.zeros((BLOCKS, 8, 128), BF16)

    for copy in smalls:
        copy.wait()

    deep = iota((BLOCKS, 128), 0)
    shift = jnp.zeros((BLOCKS, 128), F32)
    heavy = jnp.zeros((BLOCKS, 128), F32)
    for b in range(BLOCKS):
        shift = jnp.where(deep == b, shift_ref[b], shift)
        heavy = jnp.where(deep == b, weight_ref[b], heavy)
    position = (iota((BLOCKS, 128), 1) - 2).astype(F32) - shift
    coef_table[...] = sinc(position) * sinc(position / 3.0) * heavy
    coef_copy = pltpu.make_async_copy(coef_table, coef_ref, coef_sem)
    coef_copy.start()

    mine = jnp.where(owner_ref[0] == dev, 1.0, 0.0)
    lane_1 = iota((8, 128), 1)
    fit_row = jnp.zeros((8, 128), F32)
    for k in range(BASES):
        for n in range(NPOLY):
            fit_row = jnp.where(lane_1 == FIT_LANE + k * NPOLY + n, fit_ref[k, 0, n], fit_row)
    fit_row = jnp.where(mine > 0.5, fit_row, 0.0)
    fit_out[...] = fit_row
    fit_in[det] = fit_row

    lane = iota((1, ROWS), 1)
    owner_block = lane // 8
    phase = lax.rem(lane, 8)
    peer = jnp.zeros((1, ROWS), jnp.int32)
    slot = jnp.zeros((1, ROWS), jnp.int32)
    weight = jnp.zeros((1, ROWS), F32)
    for b in range(BLOCKS):
        here = owner_block == b
        goal = dest_ref[b]
        peer = jnp.where(here, (goal >> 5) & (PEERS - 1), peer)
        slot = jnp.where(here, goal & (BLOCKS - 1), slot)
        weight = jnp.where(here, weight_ref[b], weight)
    rank = jnp.zeros((1, ROWS), jnp.int32)
    for b in range(BLOCKS - 1):
        to = (dest_ref[b] >> 5) & (PEERS - 1)
        rank = rank + jnp.where(jnp.logical_and(peer == to, owner_block > b), 1, 0)
    target = rank * 128 + peer * 8 + phase
    select = jnp.where(iota((PACKED, ROWS), 0) == target, 1.0, 0.0)
    pack_mat[...] = select.astype(BF16)
    row_value = (slot * 8 + phase + 1).astype(F32)
    row_col = jnp.sum(select * row_value, axis=1, keepdims=True)
    weight_col = jnp.sum(select * weight, axis=1, keepdims=True)


    def resample(chunk):
        start = pl.multiple_of(chunk * WIDTH, 128)

        def one(block):
            source = padded[block, :, pl.ds(start, WIDTH + 256)].astype(F32)
            turn = LEAD - offset_ref[block]
            carried = iota((8, 128), 1) < turn
            turned = [
                pltpu.roll(source[:, t * 128 : (t + 1) * 128], turn, axis=1)
                for t in range(TILES + 2)
            ]
            parts = [jnp.where(carried, turned[t], turned[t + 1]) for t in range(TILES + 1)]
            return jnp.concatenate(parts, axis=1).astype(BF16)

        @pl.loop(0, BLOCKS // UNROLL)
        def _(group):
            values = [one(group * UNROLL + i) for i in range(UNROLL)]
            for i in range(UNROLL):
                moved[group * UNROLL + i] = values[i]

        for t in range(TILES):
            window = moved[:, :, t * 128 : t * 128 + 256].reshape(ROWS, 256)
            total = None
            for pair in range(3):
                pieces = jnp.dot(
                    window, shift_mat[:, pair * 256 : (pair + 1) * 256],
                    preferred_element_type=F32,
                )
                for side in range(2):
                    part = pieces[:, side * 128 : (side + 1) * 128] * coef_wide[2 * pair + side]
                    total = part if total is None else total + part
            weighted[:, t * 128 : (t + 1) * 128] = total.astype(BF16)

        gathered = jnp.dot(
            pack_mat[...], weighted[...], preferred_element_type=F32
        )
        packed[chunk] = gathered.astype(BF16).reshape(RANKS, PEERS, 8, WIDTH)

    def send(chunk):
        pltpu.make_async_copy(
            packed.at[chunk, :, pat], arrived.at[chunk, 0:RANKS, pat], bulk_recv.at[chunk]
        ).start()

        @pl.loop(1, PEERS)
        def _(step):
            other = lax.rem(pat + step, PEERS)
            pltpu.make_async_remote_copy(
                packed.at[chunk, :, other], arrived.at[chunk, 0:RANKS, pat],
                bulk_send.at[chunk], bulk_recv.at[chunk],
                device_id=(det, other), device_id_type=MESH,
            ).start()

    spot = iota((256, 768), 1)
    reads = lax.rem(spot, 128) + spot // 128 + (LEAD - 2)
    shift_mat[...] = jnp.where(iota((256, 768), 0) == reads, 1.0, 0.0).astype(BF16)
    coef_copy.wait()
    for b in range(BLOCKS):
        for i in range(6):
            coef_wide[i, b * 8 : (b + 1) * 8, :] = jnp.full((8, 128), coef_ref[b, i], F32)
    load.wait()

    resample(0)

    span = iota((8, 128), 1).astype(F32) - HALF
    norms = []
    for k in range(BASES):
        value = jnp.exp(-(span * span) / (2.0 * width_ref[k] * width_ref[k]))
        value = jnp.where(span <= HALF, value, 0.0)
        norms.append(jnp.sum(value, axis=1, keepdims=True)[0:1, :])
    across = (iota((512, 256), 0) - 128 - iota((512, 256), 1)).astype(F32)
    for k in range(BASES):
        band_mat[k] = gaussian(across, width_ref[k], norms[k]).astype(BF16)
    y_cols[...] = 2.0 * (dev * ROWS + iota((ROWS, 128), 0)).astype(F32) / (ALL_ROWS - 1) - 1.0
    for k in range(BASES):
        rowconv[k, :, 0:128] = jnp.zeros((ROWS, 128), BF16)
        rowconv[k, :, 128 + COLS :] = jnp.zeros((ROWS, 128), BF16)

    pl.semaphore_wait(barrier, PEERS - 1 + GROUPS - 1 + 2)

    @pl.loop(1, GROUPS)
    def _(step):
        pltpu.make_async_remote_copy(
            fit_out, fit_in.at[det], fit_send, fit_recv,
            device_id=(lax.rem(det + step, GROUPS), pat), device_id_type=MESH,
        ).start()

    send(0)
    whole = fit_in.at[0 : GROUPS - 1]
    pltpu.make_async_copy(whole, whole, fit_recv).wait()
    chosen = jnp.sum(fit_in[...], axis=0)
    lanes_m = iota((128, 128), 1)
    meta = jnp.broadcast_to(chosen[0:1, :], (128, 128))
    for r in range(RANKS):
        part = slice(r * 128, (r + 1) * 128)
        meta = jnp.where(lanes_m == r, row_col[part], meta)
        meta = jnp.where(lanes_m == RANKS + r, weight_col[part], meta)
    meta_out[...] = meta.reshape(PEERS, 8, 128)
    pltpu.make_async_copy(meta_out.at[pat], meta_in.at[pat], meta_recv).start()

    @pl.loop(1, PEERS)
    def _(step):
        other = lax.rem(pat + step, PEERS)
        pltpu.make_async_remote_copy(
            meta_out.at[other], meta_in.at[pat], meta_send, meta_recv,
            device_id=(det, other), device_id_type=MESH,
        ).start()

    @pl.loop(1, WINDOW)
    def _(chunk):
        resample(chunk)
        send(chunk)

    pltpu.make_async_copy(meta_in, meta_in, meta_recv).wait()
    meta_got = meta_in[...].reshape(128, 128)
    got_row = jnp.concatenate([meta_got[:, r : r + 1] for r in range(RANKS)], axis=0) - 1.0
    got_weight = jnp.concatenate(
        [meta_got[:, RANKS + r : RANKS + r + 1] for r in range(RANKS)], axis=0
    )
    lands = jnp.where(got_row == iota((PACKED, ROWS), 1).astype(F32), 1.0, 0.0)
    cover = jnp.sum(lands * got_weight, axis=0, keepdims=True)
    heads = jnp.where(got_row == (8 * iota((PACKED, 128), 1)).astype(F32), got_weight, 0.0)
    cover_ref[...] = jnp.sum(heads, axis=0, keepdims=True)[:, 0:BLOCKS]
    scale = 1.0 / jnp.maximum(cover, 1.0)
    fit_now = jnp.sum(meta_got, axis=0, keepdims=True) * 0.125
    lands = lands.astype(BF16)
    contract = (((1,), (1,)), ((), ()))
    reach = (iota((ROWS, ROWS), 1) - iota((ROWS, ROWS), 0)).astype(F32)
    rim = iota((ROWS, 2 * EDGE), 1)
    rim_at = jnp.where(rim < EDGE, rim - EDGE, rim + ROWS - EDGE)
    rim_reach = (rim_at - iota((ROWS, 2 * EDGE), 0)).astype(F32)
    low_live = jnp.where(dev > 0, 1.0, 0.0)
    high_live = jnp.where(dev < PEERS * GROUPS - 1, 1.0, 0.0)
    rim_live = jnp.where(rim < EDGE, low_live, high_live)
    for k in range(BASES):
        inner = (gaussian(reach, width_ref[k], norms[k]) * scale).astype(BF16)
        spread = lax.dot_general(inner, lands, contract, preferred_element_type=F32)
        row_mat[k * ROWS : (k + 1) * ROWS, 0:PACKED] = spread.astype(BF16)
        outer = gaussian(rim_reach, width_ref[k], norms[k]) * rim_live
        row_mat[k * ROWS : (k + 1) * ROWS, PACKED:] = outer.astype(BF16)
    edge_i = iota((2 * EDGE, ROWS), 0)
    edge_row = jnp.where(edge_i < EDGE, edge_i, edge_i + ROWS - 2 * EDGE)
    picks = jnp.where(edge_row == iota((2 * EDGE, ROWS), 1), 1.0, 0.0)
    edge_mat[...] = lax.dot_general(
        picks.astype(BF16), lands, contract, preferred_element_type=F32
    ).astype(BF16)
    edge_scale[...] = jnp.broadcast_to(
        jnp.sum(picks * scale, axis=1, keepdims=True), (2 * EDGE, 128)
    )

    def edge_copies(chunk):
        return (
            pltpu.make_async_remote_copy(
                edges.at[chunk, 0:2], arrived.at[chunk, RANKS, 2:4],
                edge_send.at[chunk], edge_recv.at[chunk],
                device_id=before_id, device_id_type=MESH,
            ),
            pltpu.make_async_remote_copy(
                edges.at[chunk, 2:4], arrived.at[chunk, RANKS, 0:2],
                edge_send.at[chunk], edge_recv.at[chunk],
                device_id=after_id, device_id_type=MESH,
            ),
        )

    def wait_bulk(chunk):
        landed = arrived.at[chunk, 0:RANKS]
        pltpu.make_async_copy(landed, landed, bulk_recv.at[chunk]).wait()

    def make_edges(chunk):
        rows = jnp.dot(
            edge_mat[...], arrived[chunk, 0:RANKS].reshape(PACKED, WIDTH),
            preferred_element_type=F32,
        )
        rows = rows * edge_scale[:, 0:1]
        edges[chunk] = rows.astype(BF16).reshape(4, 8, WIDTH)
        for copy in edge_copies(chunk):
            copy.start()

    def row_stage(chunk):
        rims = arrived.at[chunk, RANKS, 0:4]
        pltpu.make_async_copy(rims, rims, edge_recv.at[chunk]).wait()
        got = arrived[chunk, 0:RANKS].reshape(PACKED, WIDTH)
        rim_rows = arrived[chunk, RANKS, 0:4].reshape(2 * EDGE, WIDTH)
        full = jnp.concatenate([got, rim_rows], axis=0)
        at = pl.ds(pl.multiple_of(128 + chunk * WIDTH, 128), WIDTH)
        for k in range(BASES):
            value = jnp.dot(
                row_mat[k * ROWS : (k + 1) * ROWS, :], full, preferred_element_type=F32
            )
            rowconv[k, :, at] = value.astype(BF16)

    terms = [
        [
            jnp.sum(
                jnp.where(iota((1, 128), 1) == FIT_LANE + k * NPOLY + i, fit_now, 0.0),
                axis=1, keepdims=True,
            )
            for i in range(NPOLY)
        ]
        for k in range(BASES)
    ]

    def col_tile(tile):
        at = pl.multiple_of(tile * 256, 128)
        x = 2.0 * (tile * 256 + iota((1, 256), 1)).astype(F32) / (COLS - 1) - 1.0
        y = y_cols[:, 0:1]
        result = None
        for k in range(BASES):
            value = jnp.dot(
                rowconv[k, :, pl.ds(at, 512)], band_mat[k], preferred_element_type=F32
            )
            a = terms[k]
            level = a[0] + a[1] * x + a[3] * x * x
            slope = a[2] + a[4] * x
            field = level + y * slope + (a[5] * y) * y
            part = field * value
            result = part if result is None else result + part
        out_ref[:, pl.ds(at, 256)] = result.astype(BF16)

    @pl.loop(0, CHUNKS)
    def _(chunk):
        @pl.when(chunk + WINDOW < CHUNKS)
        def _():
            resample(chunk + WINDOW)

        wait_bulk(chunk)

        make_edges(chunk)

        @pl.when(chunk + WINDOW < CHUNKS)
        def _():
            send(chunk + WINDOW)

        @pl.when(chunk >= LAG)
        def _():
            row_stage(chunk - LAG)
            col_tile(2 * (chunk - LAG))

        @pl.when(chunk > LAG)
        def _():
            col_tile(2 * (chunk - LAG) - 1)

    for last in range(CHUNKS - LAG, CHUNKS):
        row_stage(last)
        col_tile(2 * last - 1)
        col_tile(2 * last)
    col_tile(2 * CHUNKS - 1)

    pltpu.make_async_copy(whole, whole, fit_send).wait()
    sent = meta_out.at[0 : PEERS - 1]
    pltpu.make_async_copy(sent, sent, meta_send).wait()

    @pl.loop(0, CHUNKS)
    def _(chunk):
        gone = packed.at[chunk, :, 0 : PEERS - 1]
        pltpu.make_async_copy(gone, gone, bulk_send.at[chunk]).wait()
        pltpu.make_async_copy(edges.at[chunk], edges.at[chunk], edge_send.at[chunk]).wait()


def shards(
    exposure, block_dest, band_offset, col_shift, block_weight, basis_width, kernel_fit, fit_owner
):
    hbm = pl.BlockSpec(memory_space=pltpu.HBM)
    smem = pl.BlockSpec(memory_space=pltpu.SMEM)
    in_hbm = functools.partial(pltpu.with_memory_space_constraint, memory_space=pltpu.HBM)
    vmem = pl.BlockSpec(memory_space=pltpu.VMEM)
    matched, cover = pl.pallas_call(
        kernel,
        out_shape=(
            jax.ShapeDtypeStruct((ROWS, COLS), BF16),
            jax.ShapeDtypeStruct((1, BLOCKS), F32),
        ),
        in_specs=[hbm] * 6 + [smem, hbm],
        out_specs=(vmem, vmem),
        scratch_shapes=[
            pltpu.SMEM((BLOCKS,), jnp.int32),
            pltpu.SMEM((BLOCKS,), jnp.int32),
            pltpu.SMEM((BLOCKS,), F32),
            pltpu.SMEM((BLOCKS,), F32),
            pltpu.SMEM((BASES,), F32),
            pltpu.SMEM((BASES, 1, NPOLY), F32),
            pltpu.SemaphoreType.DMA((6,)),
            pltpu.VMEM((BLOCKS, 8, COLS + 256), BF16),
            pltpu.VMEM((ROWS, WIDTH), BF16),
            pltpu.VMEM((CHUNKS, RANKS, PEERS, 8, WIDTH), BF16),
            pltpu.VMEM((CHUNKS, RANKS + 1, PEERS, 8, WIDTH), BF16),
            pltpu.VMEM((PEERS, 8, 128), F32),
            pltpu.VMEM((PEERS, 8, 128), F32),
            pltpu.VMEM((8, 128), F32),
            pltpu.VMEM((GROUPS, 8, 128), F32),
            pltpu.VMEM((CHUNKS, 4, 8, WIDTH), BF16),
            pltpu.VMEM((PACKED, ROWS), BF16),
            pltpu.VMEM((BASES * ROWS, PACKED + 2 * EDGE), BF16),
            pltpu.VMEM((2 * EDGE, PACKED), BF16),
            pltpu.VMEM((BASES, 512, 256), BF16),
            pltpu.VMEM((BASES, ROWS, COLS + 256), BF16),
            pltpu.VMEM((ROWS, 128), F32),
            pltpu.VMEM((2 * EDGE, 128), F32),
            pltpu.VMEM((BLOCKS, 128), F32),
            pltpu.SMEM((BLOCKS, 128), F32),
            pltpu.VMEM((BLOCKS, 8, WIDTH + 128), BF16),
            pltpu.VMEM((256, 768), BF16),
            pltpu.VMEM((6, ROWS, 128), F32),
            pltpu.SemaphoreType.DMA,
            pltpu.SemaphoreType.DMA,
            pltpu.SemaphoreType.DMA,
            pltpu.SemaphoreType.DMA,
            pltpu.SemaphoreType.DMA,
            pltpu.SemaphoreType.DMA,
            pltpu.SemaphoreType.DMA((CHUNKS,)),
            pltpu.SemaphoreType.DMA((CHUNKS,)),
            pltpu.SemaphoreType.DMA((CHUNKS,)),
            pltpu.SemaphoreType.DMA((CHUNKS,)),
        ],
        compiler_params=pltpu.CompilerParams(
            collective_id=0, has_side_effects=True, vmem_limit_bytes=32 << 20
        ),
        name="coadd_match",
    )(
        in_hbm(block_dest), in_hbm(band_offset), in_hbm(col_shift), in_hbm(block_weight),
        in_hbm(basis_width), in_hbm(kernel_fit.transpose(1, 0, 2)), fit_owner,
        in_hbm(exposure.reshape(BLOCKS, 8, COLS)),
    )
    return matched, cover.reshape(BLOCKS)


def solution(mesh):
    row_spec = P(("det", "patch"))
    in_specs = (
        P(("det", "patch"), None), row_spec, row_spec, row_spec, row_spec,
        P(), P(("det", "patch"), None, None), P(),
    )
    out_specs = (P(("det", "patch"), None), row_spec)
    return jax.shard_map(shards, mesh=mesh, in_specs=in_specs, out_specs=out_specs, check_vma=False)
```

```python
import functools

import jax
import jax.numpy as jnp
from jax import lax
from jax.experimental import pallas as pl
from jax.experimental.pallas import tpu as pltpu
from jax.sharding import PartitionSpec as P

MESH = pl.DeviceIdType.MESH
TAPS = 31
HALF = 15
BASES = 3
NPOLY = 6
COLS = 4096
CHUNKS = 8
WINDOW = 5
UNROLL = 16
LEAD = 9
FIRST = 1024
LAG = 4
WIDTH = COLS // CHUNKS
TILES = WIDTH // 128
PER = WIDTH // 256
BLOCKS = 32
ROWS = 256
PEERS = 16
GROUPS = 8
RANKS = 3
SLOTS = RANKS * PEERS
PACKED = SLOTS * 8
EDGE = 16
ALL_ROWS = ROWS * PEERS * GROUPS
FIT_LANE = 6
F32 = jnp.float32
BF16 = jnp.bfloat16


def iota(shape, dim):
    return lax.broadcasted_iota(jnp.int32, shape, dim)


def sinc(value):
    angle = jnp.pi * value
    return jnp.where(value == 0.0, 1.0, jnp.sin(angle) / jnp.where(value == 0.0, 1.0, angle))


def gaussian(distance, width, norm):
    value = jnp.exp(-(distance * distance) / (2.0 * width * width)) / norm
    return jnp.where(jnp.abs(distance) <= HALF, value, 0.0)


def kernel(
    dest_hbm, offset_hbm, shift_hbm, weight_hbm, width_hbm, fit_hbm, owner_ref, exposure_ref,
    out_ref, cover_ref,
    dest_ref, offset_ref, shift_ref, weight_ref, width_ref, fit_ref, small_sem,
    padded, weighted, packed, arrived, meta_out, meta_in, fit_out, fit_in, edges,
    pack_mat, row_mat, rim_mat, edge_mat, band_mat, rowconv, y_cols, edge_scale, coef_table,
    moved, shift_mat, coef_wide,
    load_sem, rest_sem, fit_send, fit_recv, meta_send, meta_recv, bulk_send, bulk_recv, edge_send, edge_recv,
):
    det = lax.axis_index("det")
    pat = lax.axis_index("patch")
    dev = det * PEERS + pat
    after = lax.rem(dev + 1, PEERS * GROUPS)
    before = lax.rem(dev + PEERS * GROUPS - 1, PEERS * GROUPS)
    after_id = (after // PEERS, lax.rem(after, PEERS))
    before_id = (before // PEERS, lax.rem(before, PEERS))

    smalls = [
        pltpu.make_async_copy(source, target, small_sem.at[i])
        for i, (source, target) in enumerate(
            (
                (dest_hbm, dest_ref), (shift_hbm, shift_ref), (weight_hbm, weight_ref),
                (fit_hbm, fit_ref), (offset_hbm, offset_ref),
                (width_hbm, width_ref),
            )
        )
    ]
    for copy in smalls:
        copy.start()
    load = pltpu.make_async_copy(
        exposure_ref.at[:, :, 0:FIRST], padded.at[:, :, 128 : 128 + FIRST], load_sem
    )
    load.start()
    rest = pltpu.make_async_copy(
        exposure_ref.at[:, :, FIRST:], padded.at[:, :, 128 + FIRST : 128 + COLS], rest_sem
    )
    rest.start()

    barrier = pltpu.get_barrier_semaphore()

    @pl.loop(1, PEERS)
    def _(step):
        pl.semaphore_signal(
            barrier, inc=1, device_id=(det, lax.rem(pat + step, PEERS)), device_id_type=MESH
        )

    @pl.loop(1, GROUPS)
    def _(step):
        pl.semaphore_signal(
            barrier, inc=1, device_id=(lax.rem(det + step, GROUPS), pat), device_id_type=MESH
        )

    pl.semaphore_signal(barrier, inc=1, device_id=after_id, device_id_type=MESH)
    pl.semaphore_signal(barrier, inc=1, device_id=before_id, device_id_type=MESH)

    padded[:, :, 0:128] = jnp.zeros((BLOCKS, 8, 128), BF16)
    padded[:, :, 128 + COLS :] = jnp.zeros((BLOCKS, 8, 128), BF16)

    for copy in smalls:
        copy.wait()

    deep = iota((BLOCKS, 128), 0)
    shift = jnp.zeros((BLOCKS, 128), F32)
    heavy = jnp.zeros((BLOCKS, 128), F32)
    for b in range(BLOCKS):
        shift = jnp.where(deep == b, shift_ref[b], shift)
        heavy = jnp.where(deep == b, weight_ref[b], heavy)
    position = (iota((BLOCKS, 128), 1) - 2).astype(F32) - shift
    coef_table[...] = sinc(position) * sinc(position / 3.0) * heavy

    lane = iota((1, ROWS), 1)
    owner_block = lane // 8
    phase = lax.rem(lane, 8)
    peer = jnp.zeros((1, ROWS), jnp.int32)
    slot = jnp.zeros((1, ROWS), jnp.int32)
    weight = jnp.zeros((1, ROWS), F32)
    for b in range(BLOCKS):
        here = owner_block == b
        goal = dest_ref[b]
        peer = jnp.where(here, (goal >> 5) & (PEERS - 1), peer)
        slot = jnp.where(here, goal & (BLOCKS - 1), slot)
        weight = jnp.where(here, weight_ref[b], weight)
    rank = jnp.zeros((1, ROWS), jnp.int32)
    for b in range(BLOCKS - 1):
        to = (dest_ref[b] >> 5) & (PEERS - 1)
        rank = rank + jnp.where(jnp.logical_and(peer == to, owner_block > b), 1, 0)
    target = rank * 128 + peer * 8 + phase
    select = jnp.where(iota((PACKED, ROWS), 0) == target, 1.0, 0.0)
    pack_mat[...] = select.astype(BF16)
    def resample(chunk):
        start = pl.multiple_of(chunk * WIDTH, 128)

        def one(block):
            source = padded[block, :, pl.ds(start, WIDTH + 256)].astype(F32)
            turn = LEAD - offset_ref[block]
            carried = iota((8, 128), 1) < turn
            turned = [
                pltpu.roll(source[:, t * 128 : (t + 1) * 128], turn, axis=1)
                for t in range(TILES + 2)
            ]
            parts = [jnp.where(carried, turned[t], turned[t + 1]) for t in range(TILES + 1)]
            return jnp.concatenate(parts, axis=1).astype(BF16)

        @pl.loop(0, BLOCKS // UNROLL)
        def _(group):
            values = [one(group * UNROLL + i) for i in range(UNROLL)]
            for i in range(UNROLL):
                moved[group * UNROLL + i] = values[i]

        for t in range(TILES):
            window = moved[:, :, t * 128 : t * 128 + 256].reshape(ROWS, 256)
            total = None
            for pair in range(3):
                pieces = jnp.dot(
                    window, shift_mat[:, pair * 256 : (pair + 1) * 256],
                    preferred_element_type=F32,
                )
                for side in range(2):
                    part = pieces[:, side * 128 : (side + 1) * 128] * coef_wide[2 * pair + side]
                    total = part if total is None else total + part
            weighted[:, t * 128 : (t + 1) * 128] = total.astype(BF16)

        gathered = jnp.dot(
            pack_mat[...], weighted[...], preferred_element_type=F32
        )
        packed[chunk] = gathered.astype(BF16).reshape(RANKS, PEERS, 8, WIDTH)

    def send(chunk):
        pltpu.make_async_copy(
            packed.at[chunk, :, pat], arrived.at[chunk, 0:RANKS, pat], bulk_recv.at[chunk]
        ).start()

        @pl.loop(1, PEERS)
        def _(step):
            other = lax.rem(pat + step, PEERS)
            pltpu.make_async_remote_copy(
                packed.at[chunk, :, other], arrived.at[chunk, 0:RANKS, pat],
                bulk_send.at[chunk], bulk_recv.at[chunk],
                device_id=(det, other), device_id_type=MESH,
            ).start()

    spot = iota((256, 768), 1)
    reads = lax.rem(spot, 128) + spot // 128 + (LEAD - 2)
    shift_mat[...] = jnp.where(iota((256, 768), 0) == reads, 1.0, 0.0).astype(BF16)
    for b in range(BLOCKS):
        row = jnp.broadcast_to(coef_table[b : b + 1, :], (8, 128))
        for i in range(6):
            coef_wide[i, b * 8 : (b + 1) * 8, :] = jnp.broadcast_to(row[:, i : i + 1], (8, 128))
    load.wait()

    resample(0)

    mine = jnp.where(owner_ref[0] == dev, 1.0, 0.0)
    lane_1 = iota((8, 128), 1)
    fit_row = jnp.zeros((8, 128), F32)
    for k in range(BASES):
        for n in range(NPOLY):
            fit_row = jnp.where(lane_1 == FIT_LANE + k * NPOLY + n, fit_ref[k, 0, n], fit_row)
    fit_row = jnp.where(mine > 0.5, fit_row, 0.0)
    fit_out[...] = fit_row
    fit_in[det] = fit_row

    pl.semaphore_wait(barrier, PEERS - 1 + GROUPS - 1 + 2)

    @pl.loop(1, GROUPS)
    def _(step):
        pltpu.make_async_remote_copy(
            fit_out, fit_in.at[det], fit_send, fit_recv,
            device_id=(lax.rem(det + step, GROUPS), pat), device_id_type=MESH,
        ).start()

    send(0)
    rest.wait()
    row_value = (slot * 8 + phase + 1).astype(F32)
    row_col = jnp.sum(select * row_value, axis=1, keepdims=True)
    weight_col = jnp.sum(select * weight, axis=1, keepdims=True)
    whole = fit_in.at[0 : GROUPS - 1]
    pltpu.make_async_copy(whole, whole, fit_recv).wait()
    chosen = jnp.sum(fit_in[...], axis=0)
    lanes_m = iota((128, 128), 1)
    meta = jnp.broadcast_to(chosen[0:1, :], (128, 128))
    for r in range(RANKS):
        part = slice(r * 128, (r + 1) * 128)
        meta = jnp.where(lanes_m == r, row_col[part], meta)
        meta = jnp.where(lanes_m == RANKS + r, weight_col[part], meta)
    meta_out[...] = meta.reshape(PEERS, 8, 128)
    pltpu.make_async_copy(meta_out.at[pat], meta_in.at[pat], meta_recv).start()

    @pl.loop(1, PEERS)
    def _(step):
        other = lax.rem(pat + step, PEERS)
        pltpu.make_async_remote_copy(
            meta_out.at[other], meta_in.at[pat], meta_send, meta_recv,
            device_id=(det, other), device_id_type=MESH,
        ).start()

    @pl.loop(1, WINDOW)
    def _(chunk):
        resample(chunk)
        send(chunk)

    span = iota((8, 128), 1).astype(F32) - HALF
    norms = []
    for k in range(BASES):
        value = jnp.exp(-(span * span) / (2.0 * width_ref[k] * width_ref[k]))
        value = jnp.where(span <= HALF, value, 0.0)
        norms.append(jnp.sum(value, axis=1, keepdims=True)[0:1, :])
    across = (iota((512, 256), 0) - 128 - iota((512, 256), 1)).astype(F32)
    for k in range(BASES):
        band_mat[k] = gaussian(across, width_ref[k], norms[k]).astype(BF16)
    y_cols[...] = 2.0 * (dev * ROWS + iota((ROWS, 128), 0)).astype(F32) / (ALL_ROWS - 1) - 1.0
    for k in range(BASES):
        rowconv[k, :, 0:128] = jnp.zeros((ROWS, 128), BF16)
        rowconv[k, :, 128 + COLS :] = jnp.zeros((ROWS, 128), BF16)

    pltpu.make_async_copy(meta_in, meta_in, meta_recv).wait()
    meta_got = meta_in[...].reshape(128, 128)
    got_row = jnp.concatenate([meta_got[:, r : r + 1] for r in range(RANKS)], axis=0) - 1.0
    got_weight = jnp.concatenate(
        [meta_got[:, RANKS + r : RANKS + r + 1] for r in range(RANKS)], axis=0
    )
    lands = jnp.where(got_row == iota((PACKED, ROWS), 1).astype(F32), 1.0, 0.0)
    cover = jnp.sum(lands * got_weight, axis=0, keepdims=True)
    heads = jnp.where(got_row == (8 * iota((PACKED, 128), 1)).astype(F32), got_weight, 0.0)
    cover_ref[...] = jnp.sum(heads, axis=0, keepdims=True)[:, 0:BLOCKS]
    scale = 1.0 / jnp.maximum(cover, 1.0)
    fit_now = jnp.sum(meta_got, axis=0, keepdims=True) * 0.125
    lands = lands.astype(BF16)
    contract = (((1,), (1,)), ((), ()))
    reach = (iota((ROWS, ROWS), 1) - iota((ROWS, ROWS), 0)).astype(F32)
    rim = iota((ROWS, 2 * EDGE), 1)
    rim_at = jnp.where(rim < EDGE, rim - EDGE, rim + ROWS - EDGE)
    rim_reach = (rim_at - iota((ROWS, 2 * EDGE), 0)).astype(F32)
    low_live = jnp.where(dev > 0, 1.0, 0.0)
    high_live = jnp.where(dev < PEERS * GROUPS - 1, 1.0, 0.0)
    rim_live = jnp.where(rim < EDGE, low_live, high_live)
    for k in range(BASES):
        inner = (gaussian(reach, width_ref[k], norms[k]) * scale).astype(BF16)
        spread = lax.dot_general(inner, lands, contract, preferred_element_type=F32)
        row_mat[k * ROWS : (k + 1) * ROWS, 0:PACKED] = spread.astype(BF16)
        outer = gaussian(rim_reach, width_ref[k], norms[k]) * rim_live
        for n, at in enumerate((0, ROWS - EDGE)):
            place = slice((2 * k + n) * EDGE, (2 * k + n + 1) * EDGE)
            rim_mat[place, 0:PACKED] = spread[at : at + EDGE].astype(BF16)
            rim_mat[place, PACKED:] = outer[at : at + EDGE].astype(BF16)
    edge_i = iota((2 * EDGE, ROWS), 0)
    edge_row = jnp.where(edge_i < EDGE, edge_i, edge_i + ROWS - 2 * EDGE)
    picks = jnp.where(edge_row == iota((2 * EDGE, ROWS), 1), 1.0, 0.0)
    edge_mat[...] = lax.dot_general(
        picks.astype(BF16), lands, contract, preferred_element_type=F32
    ).astype(BF16)
    edge_scale[...] = jnp.broadcast_to(
        jnp.sum(picks * scale, axis=1, keepdims=True), (2 * EDGE, 128)
    )

    def edge_copies(chunk):
        return (
            pltpu.make_async_remote_copy(
                edges.at[chunk, 0:2], arrived.at[chunk, RANKS, 2:4],
                edge_send.at[chunk], edge_recv.at[chunk],
                device_id=before_id, device_id_type=MESH,
            ),
            pltpu.make_async_remote_copy(
                edges.at[chunk, 2:4], arrived.at[chunk, RANKS, 0:2],
                edge_send.at[chunk], edge_recv.at[chunk],
                device_id=after_id, device_id_type=MESH,
            ),
        )

    def wait_bulk(chunk):
        landed = arrived.at[chunk, 0:RANKS]
        pltpu.make_async_copy(landed, landed, bulk_recv.at[chunk]).wait()

    def make_edges(chunk):
        rows = jnp.dot(
            edge_mat[...], arrived[chunk, 0:RANKS].reshape(PACKED, WIDTH),
            preferred_element_type=F32,
        )
        rows = rows * edge_scale[:, 0:1]
        edges[chunk] = rows.astype(BF16).reshape(4, 8, WIDTH)
        for copy in edge_copies(chunk):
            copy.start()

    def rims_in(chunk):
        rims = arrived.at[chunk, RANKS, 0:4]
        pltpu.make_async_copy(rims, rims, edge_recv.at[chunk]).wait()

    def columns(chunk):
        return pl.ds(pl.multiple_of(128 + chunk * WIDTH, 128), WIDTH)

    def row_stage(chunk):
        got = arrived[chunk, 0:RANKS].reshape(PACKED, WIDTH)
        for k in range(BASES):
            value = jnp.dot(
                row_mat[k * ROWS : (k + 1) * ROWS, 0:PACKED], got, preferred_element_type=F32
            )
            rowconv[k, :, columns(chunk)] = value.astype(BF16)

    def row_rims(chunk):
        got = arrived[chunk, 0:RANKS].reshape(PACKED, WIDTH)
        rim_rows = arrived[chunk, RANKS, 0:4].reshape(2 * EDGE, WIDTH)
        full = jnp.concatenate([got, rim_rows], axis=0)
        value = jnp.dot(rim_mat[...], full, preferred_element_type=F32).astype(BF16)
        for k in range(BASES):
            top = value[2 * k * EDGE : (2 * k + 1) * EDGE]
            low = value[(2 * k + 1) * EDGE : (2 * k + 2) * EDGE]
            rowconv[k, 0:EDGE, columns(chunk)] = top
            rowconv[k, ROWS - EDGE : ROWS, columns(chunk)] = low

    terms = [
        [
            jnp.sum(
                jnp.where(iota((1, 128), 1) == FIT_LANE + k * NPOLY + i, fit_now, 0.0),
                axis=1, keepdims=True,
            )
            for i in range(NPOLY)
        ]
        for k in range(BASES)
    ]

    def matched_rows(tile, y, take):
        x = 2.0 * (tile * 256 + iota((1, 256), 1)).astype(F32) / (COLS - 1) - 1.0
        result = None
        for k in range(BASES):
            value = jnp.dot(take(k), band_mat[k], preferred_element_type=F32)
            a = terms[k]
            level = a[0] + a[1] * x + a[3] * x * x
            slope = a[2] + a[4] * x
            field = level + y * slope + (a[5] * y) * y
            part = field * value
            result = part if result is None else result + part
        return result.astype(BF16)

    def col_tile(tile):
        at = pl.multiple_of(tile * 256, 128)
        out_ref[:, pl.ds(at, 256)] = matched_rows(
            tile, y_cols[:, 0:1], lambda k: rowconv[k, :, pl.ds(at, 512)]
        )

    def col_rims(tile):
        at = pl.multiple_of(tile * 256, 128)
        sides = (slice(0, EDGE), slice(ROWS - EDGE, ROWS))
        y = jnp.concatenate([y_cols[side, 0:1] for side in sides], axis=0)
        result = matched_rows(
            tile, y,
            lambda k: jnp.concatenate([rowconv[k, side, pl.ds(at, 512)] for side in sides], axis=0),
        )
        for n, side in enumerate(sides):
            out_ref[side, pl.ds(at, 256)] = result[n * EDGE : (n + 1) * EDGE]

    @pl.loop(0, CHUNKS)
    def _(chunk):
        @pl.when(chunk + WINDOW < CHUNKS)
        def _():
            resample(chunk + WINDOW)

        wait_bulk(chunk)

        make_edges(chunk)

        @pl.when(chunk + WINDOW < CHUNKS)
        def _():
            send(chunk + WINDOW)

        row_stage(chunk)

        @pl.when(chunk > 0)
        def _():
            col_tile(PER * chunk - 1)

        for back in range(PER - 1):
            col_tile(PER * chunk + back)

        @pl.when(chunk >= LAG)
        def _():
            rims_in(chunk - LAG)
            row_rims(chunk - LAG)
            for back in range(PER - 1):
                col_rims(PER * (chunk - LAG) + back)

        @pl.when(chunk > LAG)
        def _():
            col_rims(PER * (chunk - LAG) - 1)

    col_tile(PER * CHUNKS - 1)
    for last in range(CHUNKS - LAG, CHUNKS):
        rims_in(last)
        row_rims(last)
        for back in range(-1, PER - 1):
            col_rims(PER * last + back)
    col_rims(PER * CHUNKS - 1)

    pltpu.make_async_copy(whole, whole, fit_send).wait()
    sent = meta_out.at[0 : PEERS - 1]
    pltpu.make_async_copy(sent, sent, meta_send).wait()

    @pl.loop(0, CHUNKS)
    def _(chunk):
        gone = packed.at[chunk, :, 0 : PEERS - 1]
        pltpu.make_async_copy(gone, gone, bulk_send.at[chunk]).wait()
        pltpu.make_async_copy(edges.at[chunk], edges.at[chunk], edge_send.at[chunk]).wait()


def shards(
    exposure, block_dest, band_offset, col_shift, block_weight, basis_width, kernel_fit, fit_owner
):
    hbm = pl.BlockSpec(memory_space=pltpu.HBM)
    smem = pl.BlockSpec(memory_space=pltpu.SMEM)
    in_hbm = functools.partial(pltpu.with_memory_space_constraint, memory_space=pltpu.HBM)
    vmem = pl.BlockSpec(memory_space=pltpu.VMEM)
    matched, cover = pl.pallas_call(
        kernel,
        out_shape=(
            jax.ShapeDtypeStruct((ROWS, COLS), BF16),
            jax.ShapeDtypeStruct((1, BLOCKS), F32),
        ),
        in_specs=[hbm] * 6 + [smem, hbm],
        out_specs=(vmem, vmem),
        scratch_shapes=[
            pltpu.SMEM((BLOCKS,), jnp.int32),
            pltpu.SMEM((BLOCKS,), jnp.int32),
            pltpu.SMEM((BLOCKS,), F32),
            pltpu.SMEM((BLOCKS,), F32),
            pltpu.SMEM((BASES,), F32),
            pltpu.SMEM((BASES, 1, NPOLY), F32),
            pltpu.SemaphoreType.DMA((6,)),
            pltpu.VMEM((BLOCKS, 8, COLS + 256), BF16),
            pltpu.VMEM((ROWS, WIDTH), BF16),
            pltpu.VMEM((CHUNKS, RANKS, PEERS, 8, WIDTH), BF16),
            pltpu.VMEM((CHUNKS, RANKS + 1, PEERS, 8, WIDTH), BF16),
            pltpu.VMEM((PEERS, 8, 128), F32),
            pltpu.VMEM((PEERS, 8, 128), F32),
            pltpu.VMEM((8, 128), F32),
            pltpu.VMEM((GROUPS, 8, 128), F32),
            pltpu.VMEM((CHUNKS, 4, 8, WIDTH), BF16),
            pltpu.VMEM((PACKED, ROWS), BF16),
            pltpu.VMEM((BASES * ROWS, PACKED), BF16),
            pltpu.VMEM((BASES * 2 * EDGE, PACKED + 2 * EDGE), BF16),
            pltpu.VMEM((2 * EDGE, PACKED), BF16),
            pltpu.VMEM((BASES, 512, 256), BF16),
            pltpu.VMEM((BASES, ROWS, COLS + 256), BF16),
            pltpu.VMEM((ROWS, 128), F32),
            pltpu.VMEM((2 * EDGE, 128), F32),
            pltpu.VMEM((BLOCKS, 128), F32),
            pltpu.VMEM((BLOCKS, 8, WIDTH + 128), BF16),
            pltpu.VMEM((256, 768), BF16),
            pltpu.VMEM((6, ROWS, 128), F32),
            pltpu.SemaphoreType.DMA,
            pltpu.SemaphoreType.DMA,
            pltpu.SemaphoreType.DMA,
            pltpu.SemaphoreType.DMA,
            pltpu.SemaphoreType.DMA,
            pltpu.SemaphoreType.DMA,
            pltpu.SemaphoreType.DMA((CHUNKS,)),
            pltpu.SemaphoreType.DMA((CHUNKS,)),
            pltpu.SemaphoreType.DMA((CHUNKS,)),
            pltpu.SemaphoreType.DMA((CHUNKS,)),
        ],
        compiler_params=pltpu.CompilerParams(
            collective_id=0, has_side_effects=True, vmem_limit_bytes=32 << 20
        ),
        name="coadd_match",
    )(
        in_hbm(block_dest), in_hbm(band_offset), in_hbm(col_shift), in_hbm(block_weight),
        in_hbm(basis_width), in_hbm(kernel_fit.transpose(1, 0, 2)), fit_owner,
        in_hbm(exposure.reshape(BLOCKS, 8, COLS)),
    )
    return matched, cover.reshape(BLOCKS)


def solution(mesh):
    row_spec = P(("det", "patch"))
    in_specs = (
        P(("det", "patch"), None), row_spec, row_spec, row_spec, row_spec,
        P(), P(("det", "patch"), None, None), P(),
    )
    out_specs = (P(("det", "patch"), None), row_spec)
    return jax.shard_map(shards, mesh=mesh, in_specs=in_specs, out_specs=out_specs, check_vma=False)
```

```python
import functools

import jax
import jax.numpy as jnp
from jax import lax
from jax.experimental import pallas as pl
from jax.experimental.pallas import tpu as pltpu
from jax.sharding import PartitionSpec as P

MESH = pl.DeviceIdType.MESH
TAPS = 31
HALF = 15
BASES = 3
NPOLY = 6
COLS = 4096
CHUNKS = 8
WINDOW = 5
UNROLL = 16
LEAD = 9
FIRST = 1024
LAG = 4
WIDTH = COLS // CHUNKS
TILES = WIDTH // 128
PER = WIDTH // 256
BLOCKS = 32
ROWS = 256
PEERS = 16
GROUPS = 8
RANKS = 3
SLOTS = RANKS * PEERS
PACKED = SLOTS * 8
EDGE = 16
ALL_ROWS = ROWS * PEERS * GROUPS
FIT_LANE = 6
F32 = jnp.float32
BF16 = jnp.bfloat16


def iota(shape, dim):
    return lax.broadcasted_iota(jnp.int32, shape, dim)


def sinc(value):
    angle = jnp.pi * value
    return jnp.where(value == 0.0, 1.0, jnp.sin(angle) / jnp.where(value == 0.0, 1.0, angle))


def gaussian(distance, width, norm):
    value = jnp.exp(-(distance * distance) / (2.0 * width * width)) / norm
    return jnp.where(jnp.abs(distance) <= HALF, value, 0.0)


def kernel(
    dest_hbm, offset_hbm, shift_hbm, weight_hbm, width_hbm, fit_hbm, owner_ref, exposure_ref,
    out_ref, cover_ref,
    dest_ref, offset_ref, shift_ref, weight_ref, width_ref, fit_ref, small_sem,
    padded, weighted, packed, arrived, meta_out, meta_in, fit_out, fit_in, edges,
    pack_mat, row_mat, rim_mat, edge_mat, band_mat, rowconv, y_cols, edge_scale, coef_table,
    moved, shift_mat, coef_wide,
    load_sem, rest_sem, fit_send, fit_recv, meta_send, meta_recv, bulk_send, bulk_recv, edge_send, edge_recv,
):
    det = lax.axis_index("det")
    pat = lax.axis_index("patch")
    dev = det * PEERS + pat
    after = lax.rem(dev + 1, PEERS * GROUPS)
    before = lax.rem(dev + PEERS * GROUPS - 1, PEERS * GROUPS)
    after_id = (after // PEERS, lax.rem(after, PEERS))
    before_id = (before // PEERS, lax.rem(before, PEERS))

    smalls = [
        pltpu.make_async_copy(source, target, small_sem.at[i])
        for i, (source, target) in enumerate(
            (
                (dest_hbm, dest_ref), (shift_hbm, shift_ref), (weight_hbm, weight_ref),
                (fit_hbm, fit_ref), (offset_hbm, offset_ref),
                (width_hbm, width_ref),
            )
        )
    ]
    for copy in smalls:
        copy.start()
    load = pltpu.make_async_copy(
        exposure_ref.at[:, :, 0:FIRST], padded.at[:, :, 128 : 128 + FIRST], load_sem
    )
    load.start()
    rest = pltpu.make_async_copy(
        exposure_ref.at[:, :, FIRST:], padded.at[:, :, 128 + FIRST : 128 + COLS], rest_sem
    )
    rest.start()

    barrier = pltpu.get_barrier_semaphore()

    @pl.loop(1, PEERS)
    def _(step):
        pl.semaphore_signal(
            barrier, inc=1, device_id=(det, lax.rem(pat + step, PEERS)), device_id_type=MESH
        )

    @pl.loop(1, GROUPS)
    def _(step):
        pl.semaphore_signal(
            barrier, inc=1, device_id=(lax.rem(det + step, GROUPS), pat), device_id_type=MESH
        )

    pl.semaphore_signal(barrier, inc=1, device_id=after_id, device_id_type=MESH)
    pl.semaphore_signal(barrier, inc=1, device_id=before_id, device_id_type=MESH)

    padded[:, :, 0:128] = jnp.zeros((BLOCKS, 8, 128), BF16)
    padded[:, :, 128 + COLS :] = jnp.zeros((BLOCKS, 8, 128), BF16)

    for copy in smalls:
        copy.wait()

    deep = iota((BLOCKS, 128), 0)
    shift = jnp.zeros((BLOCKS, 128), F32)
    heavy = jnp.zeros((BLOCKS, 128), F32)
    for b in range(BLOCKS):
        shift = jnp.where(deep == b, shift_ref[b], shift)
        heavy = jnp.where(deep == b, weight_ref[b], heavy)
    position = (iota((BLOCKS, 128), 1) - 2).astype(F32) - shift
    coef_table[...] = sinc(position) * sinc(position / 3.0) * heavy

    lane = iota((1, ROWS), 1)
    owner_block = lane // 8
    phase = lax.rem(lane, 8)
    peer = jnp.zeros((1, ROWS), jnp.int32)
    slot = jnp.zeros((1, ROWS), jnp.int32)
    weight = jnp.zeros((1, ROWS), F32)
    for b in range(BLOCKS):
        here = owner_block == b
        goal = dest_ref[b]
        peer = jnp.where(here, (goal >> 5) & (PEERS - 1), peer)
        slot = jnp.where(here, goal & (BLOCKS - 1), slot)
        weight = jnp.where(here, weight_ref[b], weight)
    rank = jnp.zeros((1, ROWS), jnp.int32)
    for b in range(BLOCKS - 1):
        to = (dest_ref[b] >> 5) & (PEERS - 1)
        rank = rank + jnp.where(jnp.logical_and(peer == to, owner_block > b), 1, 0)
    target = rank * 128 + peer * 8 + phase
    select = jnp.where(iota((PACKED, ROWS), 0) == target, 1.0, 0.0)
    pack_mat[...] = select.astype(BF16)
    def resample(chunk):
        start = pl.multiple_of(chunk * WIDTH, 128)

        def one(block):
            source = padded[block, :, pl.ds(start, WIDTH + 256)].astype(F32)
            turn = LEAD - offset_ref[block]
            carried = iota((8, 128), 1) < turn
            turned = [
                pltpu.roll(source[:, t * 128 : (t + 1) * 128], turn, axis=1)
                for t in range(TILES + 2)
            ]
            parts = [jnp.where(carried, turned[t], turned[t + 1]) for t in range(TILES + 1)]
            return jnp.concatenate(parts, axis=1).astype(BF16)

        @pl.loop(0, BLOCKS // UNROLL)
        def _(group):
            values = [one(group * UNROLL + i) for i in range(UNROLL)]
            for i in range(UNROLL):
                moved[group * UNROLL + i] = values[i]

        for t in range(TILES):
            window = moved[:, :, t * 128 : t * 128 + 256].reshape(ROWS, 256)
            total = None
            for pair in range(3):
                pieces = jnp.dot(
                    window, shift_mat[:, pair * 256 : (pair + 1) * 256],
                    preferred_element_type=F32,
                )
                for side in range(2):
                    part = pieces[:, side * 128 : (side + 1) * 128] * coef_wide[2 * pair + side]
                    total = part if total is None else total + part
            weighted[:, t * 128 : (t + 1) * 128] = total.astype(BF16)

        gathered = jnp.dot(
            pack_mat[...], weighted[...], preferred_element_type=F32
        )
        packed[chunk] = gathered.astype(BF16).reshape(RANKS, PEERS, 8, WIDTH)

    def send(chunk):
        pltpu.make_async_copy(
            packed.at[chunk, :, pat], arrived.at[chunk, 0:RANKS, pat], bulk_recv.at[chunk]
        ).start()

        @pl.loop(1, PEERS)
        def _(step):
            other = lax.rem(pat + step, PEERS)
            pltpu.make_async_remote_copy(
                packed.at[chunk, :, other], arrived.at[chunk, 0:RANKS, pat],
                bulk_send.at[chunk], bulk_recv.at[chunk],
                device_id=(det, other), device_id_type=MESH,
            ).start()

    spot = iota((256, 768), 1)
    reads = lax.rem(spot, 128) + spot // 128 + (LEAD - 2)
    shift_mat[...] = jnp.where(iota((256, 768), 0) == reads, 1.0, 0.0).astype(BF16)
    for b in range(BLOCKS):
        row = jnp.broadcast_to(coef_table[b : b + 1, :], (8, 128))
        for i in range(6):
            coef_wide[i, b * 8 : (b + 1) * 8, :] = jnp.broadcast_to(row[:, i : i + 1], (8, 128))
    load.wait()

    resample(0)

    mine = jnp.where(owner_ref[0] == dev, 1.0, 0.0)
    lane_1 = iota((8, 128), 1)
    fit_row = jnp.zeros((8, 128), F32)
    for k in range(BASES):
        for n in range(NPOLY):
            fit_row = jnp.where(lane_1 == FIT_LANE + k * NPOLY + n, fit_ref[k, 0, n], fit_row)
    fit_row = jnp.where(mine > 0.5, fit_row, 0.0)
    fit_out[...] = fit_row
    fit_in[det] = fit_row

    pl.semaphore_wait(barrier, PEERS - 1 + GROUPS - 1 + 2)

    @pl.loop(1, GROUPS)
    def _(step):
        pltpu.make_async_remote_copy(
            fit_out, fit_in.at[det], fit_send, fit_recv,
            device_id=(lax.rem(det + step, GROUPS), pat), device_id_type=MESH,
        ).start()

    send(0)
    rest.wait()
    row_value = (slot * 8 + phase + 1).astype(F32)
    row_col = jnp.sum(select * row_value, axis=1, keepdims=True)
    weight_col = jnp.sum(select * weight, axis=1, keepdims=True)
    whole = fit_in.at[0 : GROUPS - 1]
    pltpu.make_async_copy(whole, whole, fit_recv).wait()
    chosen = jnp.sum(fit_in[...], axis=0)
    lanes_m = iota((128, 128), 1)
    meta = jnp.broadcast_to(chosen[0:1, :], (128, 128))
    for r in range(RANKS):
        part = slice(r * 128, (r + 1) * 128)
        meta = jnp.where(lanes_m == r, row_col[part], meta)
        meta = jnp.where(lanes_m == RANKS + r, weight_col[part], meta)
    meta_out[...] = meta.reshape(PEERS, 8, 128)
    pltpu.make_async_copy(meta_out.at[pat], meta_in.at[pat], meta_recv).start()

    @pl.loop(1, PEERS)
    def _(step):
        other = lax.rem(pat + step, PEERS)
        pltpu.make_async_remote_copy(
            meta_out.at[other], meta_in.at[pat], meta_send, meta_recv,
            device_id=(det, other), device_id_type=MESH,
        ).start()

    @pl.loop(1, WINDOW)
    def _(chunk):
        resample(chunk)
        send(chunk)

    span = iota((8, 128), 1).astype(F32) - HALF
    norms = []
    for k in range(BASES):
        value = jnp.exp(-(span * span) / (2.0 * width_ref[k] * width_ref[k]))
        value = jnp.where(span <= HALF, value, 0.0)
        norms.append(jnp.sum(value, axis=1, keepdims=True)[0:1, :])
    across = (iota((512, 256), 0) - 128 - iota((512, 256), 1)).astype(F32)
    for k in range(BASES):
        band_mat[k] = gaussian(across, width_ref[k], norms[k]).astype(BF16)
    y_cols[...] = 2.0 * (dev * ROWS + iota((ROWS, 128), 0)).astype(F32) / (ALL_ROWS - 1) - 1.0
    for k in range(BASES):
        rowconv[k, :, 0:128] = jnp.zeros((ROWS, 128), BF16)
        rowconv[k, :, 128 + COLS :] = jnp.zeros((ROWS, 128), BF16)

    pltpu.make_async_copy(meta_in, meta_in, meta_recv).wait()
    meta_got = meta_in[...].reshape(128, 128)
    got_row = jnp.concatenate([meta_got[:, r : r + 1] for r in range(RANKS)], axis=0) - 1.0
    got_weight = jnp.concatenate(
        [meta_got[:, RANKS + r : RANKS + r + 1] for r in range(RANKS)], axis=0
    )
    lands = jnp.where(got_row == iota((PACKED, ROWS), 1).astype(F32), 1.0, 0.0)
    cover = jnp.sum(lands * got_weight, axis=0, keepdims=True)
    heads = jnp.where(got_row == (8 * iota((PACKED, 128), 1)).astype(F32), got_weight, 0.0)
    cover_ref[...] = jnp.sum(heads, axis=0, keepdims=True)[:, 0:BLOCKS]
    scale = 1.0 / jnp.maximum(cover, 1.0)
    fit_now = jnp.sum(meta_got, axis=0, keepdims=True) * 0.125
    lands = lands.astype(BF16)
    contract = (((1,), (1,)), ((), ()))
    reach = (iota((ROWS, ROWS), 1) - iota((ROWS, ROWS), 0)).astype(F32)
    rim = iota((ROWS, 2 * EDGE), 1)
    rim_at = jnp.where(rim < EDGE, rim - EDGE, rim + ROWS - EDGE)
    rim_reach = (rim_at - iota((ROWS, 2 * EDGE), 0)).astype(F32)
    low_live = jnp.where(dev > 0, 1.0, 0.0)
    high_live = jnp.where(dev < PEERS * GROUPS - 1, 1.0, 0.0)
    rim_live = jnp.where(rim < EDGE, low_live, high_live)
    for k in range(BASES):
        inner = (gaussian(reach, width_ref[k], norms[k]) * scale).astype(BF16)
        spread = lax.dot_general(inner, lands, contract, preferred_element_type=F32)
        row_mat[k * ROWS : (k + 1) * ROWS, 0:PACKED] = spread.astype(BF16)
        outer = gaussian(rim_reach, width_ref[k], norms[k]) * rim_live
        for n, at in enumerate((0, ROWS - EDGE)):
            place = slice((2 * k + n) * EDGE, (2 * k + n + 1) * EDGE)
            rim_mat[place, 0:PACKED] = spread[at : at + EDGE].astype(BF16)
            rim_mat[place, PACKED:] = outer[at : at + EDGE].astype(BF16)
    edge_i = iota((2 * EDGE, ROWS), 0)
    edge_row = jnp.where(edge_i < EDGE, edge_i, edge_i + ROWS - 2 * EDGE)
    picks = jnp.where(edge_row == iota((2 * EDGE, ROWS), 1), 1.0, 0.0)
    edge_mat[...] = lax.dot_general(
        picks.astype(BF16), lands, contract, preferred_element_type=F32
    ).astype(BF16)
    edge_scale[...] = jnp.broadcast_to(
        jnp.sum(picks * scale, axis=1, keepdims=True), (2 * EDGE, 128)
    )

    def edge_copies(chunk):
        return (
            pltpu.make_async_remote_copy(
                edges.at[chunk, 0:2], arrived.at[chunk, RANKS, 2:4],
                edge_send.at[chunk], edge_recv.at[chunk],
                device_id=before_id, device_id_type=MESH,
            ),
            pltpu.make_async_remote_copy(
                edges.at[chunk, 2:4], arrived.at[chunk, RANKS, 0:2],
                edge_send.at[chunk], edge_recv.at[chunk],
                device_id=after_id, device_id_type=MESH,
            ),
        )

    def wait_bulk(chunk):
        landed = arrived.at[chunk, 0:RANKS]
        pltpu.make_async_copy(landed, landed, bulk_recv.at[chunk]).wait()

    def make_edges(chunk):
        rows = jnp.dot(
            edge_mat[...], arrived[chunk, 0:RANKS].reshape(PACKED, WIDTH),
            preferred_element_type=F32,
        )
        rows = rows * edge_scale[:, 0:1]
        edges[chunk] = rows.astype(BF16).reshape(4, 8, WIDTH)
        for copy in edge_copies(chunk):
            copy.start()

    def rims_in(chunk):
        rims = arrived.at[chunk, RANKS, 0:4]
        pltpu.make_async_copy(rims, rims, edge_recv.at[chunk]).wait()

    def columns(chunk):
        return pl.ds(pl.multiple_of(128 + chunk * WIDTH, 128), WIDTH)

    def row_stage(chunk):
        got = arrived[chunk, 0:RANKS].reshape(PACKED, WIDTH)
        for k in range(BASES):
            value = jnp.dot(
                row_mat[k * ROWS : (k + 1) * ROWS, 0:PACKED], got, preferred_element_type=F32
            )
            rowconv[k, :, columns(chunk)] = value.astype(BF16)

    def row_rims(chunk):
        got = arrived[chunk, 0:RANKS].reshape(PACKED, WIDTH)
        rim_rows = arrived[chunk, RANKS, 0:4].reshape(2 * EDGE, WIDTH)
        full = jnp.concatenate([got, rim_rows], axis=0)
        value = jnp.dot(rim_mat[...], full, preferred_element_type=F32).astype(BF16)
        for k in range(BASES):
            top = value[2 * k * EDGE : (2 * k + 1) * EDGE]
            low = value[(2 * k + 1) * EDGE : (2 * k + 2) * EDGE]
            rowconv[k, 0:EDGE, columns(chunk)] = top
            rowconv[k, ROWS - EDGE : ROWS, columns(chunk)] = low

    terms = [
        [
            jnp.sum(
                jnp.where(iota((1, 128), 1) == FIT_LANE + k * NPOLY + i, fit_now, 0.0),
                axis=1, keepdims=True,
            )
            for i in range(NPOLY)
        ]
        for k in range(BASES)
    ]

    def matched_rows(tile, y, take):
        x = 2.0 * (tile * 256 + iota((1, 256), 1)).astype(F32) / (COLS - 1) - 1.0
        result = None
        for k in range(BASES):
            value = jnp.dot(take(k), band_mat[k], preferred_element_type=F32)
            a = terms[k]
            level = a[0] + a[1] * x + a[3] * x * x
            slope = a[2] + a[4] * x
            field = level + y * slope + (a[5] * y) * y
            part = field * value
            result = part if result is None else result + part
        return result.astype(BF16)

    def col_tile(tile):
        at = pl.multiple_of(tile * 256, 128)
        out_ref[:, pl.ds(at, 256)] = matched_rows(
            tile, y_cols[:, 0:1], lambda k: rowconv[k, :, pl.ds(at, 512)]
        )

    def col_rims(tile):
        at = pl.multiple_of(tile * 256, 128)
        sides = (slice(0, EDGE), slice(ROWS - EDGE, ROWS))
        y = jnp.concatenate([y_cols[side, 0:1] for side in sides], axis=0)
        result = matched_rows(
            tile, y,
            lambda k: jnp.concatenate([rowconv[k, side, pl.ds(at, 512)] for side in sides], axis=0),
        )
        for n, side in enumerate(sides):
            out_ref[side, pl.ds(at, 256)] = result[n * EDGE : (n + 1) * EDGE]

    @pl.loop(0, CHUNKS)
    def _(chunk):
        wait_bulk(chunk)

        make_edges(chunk)

        @pl.when(chunk + WINDOW < CHUNKS)
        def _():
            resample(chunk + WINDOW)

        @pl.when(chunk + WINDOW < CHUNKS)
        def _():
            send(chunk + WINDOW)

        row_stage(chunk)

        @pl.when(chunk > 0)
        def _():
            col_tile(PER * chunk - 1)

        for back in range(PER - 1):
            col_tile(PER * chunk + back)

        @pl.when(chunk >= LAG)
        def _():
            rims_in(chunk - LAG)
            row_rims(chunk - LAG)
            for back in range(PER - 1):
                col_rims(PER * (chunk - LAG) + back)

        @pl.when(chunk > LAG)
        def _():
            col_rims(PER * (chunk - LAG) - 1)

    col_tile(PER * CHUNKS - 1)
    for last in range(CHUNKS - LAG, CHUNKS):
        rims_in(last)
        row_rims(last)
        for back in range(-1, PER - 1):
            col_rims(PER * last + back)
    col_rims(PER * CHUNKS - 1)

    pltpu.make_async_copy(whole, whole, fit_send).wait()
    sent = meta_out.at[0 : PEERS - 1]
    pltpu.make_async_copy(sent, sent, meta_send).wait()

    @pl.loop(0, CHUNKS)
    def _(chunk):
        gone = packed.at[chunk, :, 0 : PEERS - 1]
        pltpu.make_async_copy(gone, gone, bulk_send.at[chunk]).wait()
        pltpu.make_async_copy(edges.at[chunk], edges.at[chunk], edge_send.at[chunk]).wait()


def shards(
    exposure, block_dest, band_offset, col_shift, block_weight, basis_width, kernel_fit, fit_owner
):
    hbm = pl.BlockSpec(memory_space=pltpu.HBM)
    smem = pl.BlockSpec(memory_space=pltpu.SMEM)
    in_hbm = functools.partial(pltpu.with_memory_space_constraint, memory_space=pltpu.HBM)
    vmem = pl.BlockSpec(memory_space=pltpu.VMEM)
    matched, cover = pl.pallas_call(
        kernel,
        out_shape=(
            jax.ShapeDtypeStruct((ROWS, COLS), BF16),
            jax.ShapeDtypeStruct((1, BLOCKS), F32),
        ),
        in_specs=[hbm] * 6 + [smem, hbm],
        out_specs=(vmem, vmem),
        scratch_shapes=[
            pltpu.SMEM((BLOCKS,), jnp.int32),
            pltpu.SMEM((BLOCKS,), jnp.int32),
            pltpu.SMEM((BLOCKS,), F32),
            pltpu.SMEM((BLOCKS,), F32),
            pltpu.SMEM((BASES,), F32),
            pltpu.SMEM((BASES, 1, NPOLY), F32),
            pltpu.SemaphoreType.DMA((6,)),
            pltpu.VMEM((BLOCKS, 8, COLS + 256), BF16),
            pltpu.VMEM((ROWS, WIDTH), BF16),
            pltpu.VMEM((CHUNKS, RANKS, PEERS, 8, WIDTH), BF16),
            pltpu.VMEM((CHUNKS, RANKS + 1, PEERS, 8, WIDTH), BF16),
            pltpu.VMEM((PEERS, 8, 128), F32),
            pltpu.VMEM((PEERS, 8, 128), F32),
            pltpu.VMEM((8, 128), F32),
            pltpu.VMEM((GROUPS, 8, 128), F32),
            pltpu.VMEM((CHUNKS, 4, 8, WIDTH), BF16),
            pltpu.VMEM((PACKED, ROWS), BF16),
            pltpu.VMEM((BASES * ROWS, PACKED), BF16),
            pltpu.VMEM((BASES * 2 * EDGE, PACKED + 2 * EDGE), BF16),
            pltpu.VMEM((2 * EDGE, PACKED), BF16),
            pltpu.VMEM((BASES, 512, 256), BF16),
            pltpu.VMEM((BASES, ROWS, COLS + 256), BF16),
            pltpu.VMEM((ROWS, 128), F32),
            pltpu.VMEM((2 * EDGE, 128), F32),
            pltpu.VMEM((BLOCKS, 128), F32),
            pltpu.VMEM((BLOCKS, 8, WIDTH + 128), BF16),
            pltpu.VMEM((256, 768), BF16),
            pltpu.VMEM((6, ROWS, 128), F32),
            pltpu.SemaphoreType.DMA,
            pltpu.SemaphoreType.DMA,
            pltpu.SemaphoreType.DMA,
            pltpu.SemaphoreType.DMA,
            pltpu.SemaphoreType.DMA,
            pltpu.SemaphoreType.DMA,
            pltpu.SemaphoreType.DMA((CHUNKS,)),
            pltpu.SemaphoreType.DMA((CHUNKS,)),
            pltpu.SemaphoreType.DMA((CHUNKS,)),
            pltpu.SemaphoreType.DMA((CHUNKS,)),
        ],
        compiler_params=pltpu.CompilerParams(
            collective_id=0, has_side_effects=True, vmem_limit_bytes=32 << 20
        ),
        name="coadd_match",
    )(
        in_hbm(block_dest), in_hbm(band_offset), in_hbm(col_shift), in_hbm(block_weight),
        in_hbm(basis_width), in_hbm(kernel_fit.transpose(1, 0, 2)), fit_owner,
        in_hbm(exposure.reshape(BLOCKS, 8, COLS)),
    )
    return matched, cover.reshape(BLOCKS)


def solution(mesh):
    row_spec = P(("det", "patch"))
    in_specs = (
        P(("det", "patch"), None), row_spec, row_spec, row_spec, row_spec,
        P(), P(("det", "patch"), None, None), P(),
    )
    out_specs = (P(("det", "patch"), None), row_spec)
    return jax.shard_map(shards, mesh=mesh, in_specs=in_specs, out_specs=out_specs, check_vma=False)
```
